32 devices in a mesh: scene: 2 (over y), seq: 4 (over z), head: 2 (over x), band: 2 (over core).
Axes of the slice: x: 2, y: 2, z: 4, core: 2. Of those that a mesh axis runs over, the one named last changes fastest.
Arguments:
- tokens: bfloat16 [8, 12, 37, 1024], P(('scene', 'seq'), ('head', 'band')), parts along dimension 0, may hold values from -6 to 6
- frame_gain: float32 [1024], replicated, may hold values from 0.5 to 1.5
- frame_qkv: bfloat16 [3, 1024, 1024], P(None, None, 'head'), may hold values from -6 to 6
- frame_out: bfloat16 [1024, 1024], P('head'), may hold values from -0.1875 to 0.1875
- global_gain: float32 [1024], replicated, may hold values from 0.5 to 1.5
- global_qkv: bfloat16 [3, 1024, 1024], P(None, None, 'head'), may hold values from -6 to 6
- global_out: bfloat16 [1024, 1024], P('head'), may hold values from -0.1875 to 0.1875
- head_gain: float32 [2048], replicated, may hold values from 0.5 to 1.5
- head_proj: bfloat16 [2048, 256], replicated, may hold values from -0.125 to 0.125
- head_bias: float32 [256], replicated, may hold values from -3 to 3
- head_conv: bfloat16 [3, 3, 256, 256], replicated, may hold values from -0.125 to 0.125
Outputs:
- blocks: bfloat16 [8, 12, 37, 1024], P(('scene', 'seq'), ('head', 'band')), parts along dimension 0
- features: bfloat16 [8, 12, 37, 256], P(('scene', 'seq'), ('head', 'band')), parts along dimension 0
The draws below stay inside these ranges and needn't reach their ends.
There are 2 independent parts, one for each index of `scene`. The reference program is written for one: setup_inputs(seed, part) draws one part's arguments, and reference() takes and returns one part's arrays. A program takes and returns all parts, laid end to end along the dimension named above; an argument that names none is the same for every part. Nothing has to cross between parts.
All inputs are finite; a program needn't handle non-finite values.
Results may differ from the reference program's by a relative error of at most 0.017.
Values may be sent and summed in bfloat16 or wider, within the bound.
A program may use at most 256 MiB of HBM per device.

```python
import math
import jax
import jax.numpy as jnp
from jax import lax

D = 1024
HEADS = 16
HD = 64
CH = 256
PC = 37
PR = 12
FRAMES = 4


def projection_draw(key):
    first_key, second_key = jax.random.split(key, 2)
    base = jax.random.truncated_normal(first_key, -6.0, 6.0, (3, D, D), jnp.float32) * D ** (-0.5)
    head_scale = jnp.exp(jax.random.uniform(second_key, (2, HEADS), jnp.float32, math.log(1.3), math.log(2.2)))
    columns = jnp.repeat(head_scale, HD, axis=1)
    queries = base[0] * columns[0]
    keys_part = base[1] * columns[1]
    stacked = jnp.stack([queries, keys_part, base[2]])
    return jnp.clip(stacked, -6.0, 6.0).astype(jnp.bfloat16)


def draw_frame_qkv(key, part):
    return projection_draw(jax.random.fold_in(key, 11))


def draw_global_qkv(key, part):
    return projection_draw(jax.random.fold_in(key, 23))


def level_of(key, shape, cuts, low, largest):
    level, own = 1.0, jax.random.fold_in(key, 6)
    for axis_at, blocks in cuts:
        heights = jnp.exp(jax.random.uniform(jax.random.fold_in(own, axis_at), (blocks,), jnp.float32, low / len(cuts), largest / len(cuts)))
        level = level * jnp.repeat(heights, shape[axis_at] // blocks).reshape([-1 if axis == axis_at else 1 for axis in range(len(shape))])
    return level


def noise(own_key, shape, scale, most, shards=(), held_as=jnp.bfloat16):
    values = jax.random.normal(own_key, shape, jnp.float32) * scale
    if len(shards) > 0:
        values = level_of(own_key, shape, shards, -0.22, 0.18) * values
    return jnp.clip(values, min=-most, max=most).astype(held_as)


def setup_inputs(seed: int = 0, part: int = 0) -> dict:
    key_of = jax.random.split(jax.random.key(seed), 12)
    own_keys = jax.random.split(jax.random.fold_in(key_of[11], part), 12)
    tokens = noise(own_keys[0], (FRAMES, PR, PC, D), 1.0, 6.0, ((0, 4), (1, 4)))
    frame_gain = jnp.clip(1.0 + 0.1 * jax.random.normal(key_of[1], (D,), jnp.float32), 0.5, 1.5)
    frame_qkv = draw_frame_qkv(jax.random.fold_in(key_of[11], 71), part)
    frame_out = noise(key_of[3], (D, D), D ** -0.5, 0.1875, ((0, 2),))
    global_gain = jnp.clip(1.0 + 0.1 * jax.random.normal(key_of[4], (D,), jnp.float32), 0.5, 1.5)
    global_qkv = draw_global_qkv(jax.random.fold_in(key_of[11], 71), part)
    global_out = noise(key_of[6], (D, D), D ** -0.5, 0.1875, ((0, 2),))
    head_gain = jnp.clip(1.0 + 0.1 * jax.random.normal(key_of[7], (2 * D,), jnp.float32), 0.5, 1.5)
    head_proj = noise(key_of[8], (2 * D, CH), (2 * D) ** -0.5, 0.125)
    head_bias = noise(key_of[9], (CH,), 0.5, 3.0, (), jnp.float32)
    head_conv = noise(key_of[10], (3, 3, CH, CH), (9 * CH) ** -0.5, 0.125)
    return {"tokens": tokens, "frame_gain": frame_gain, "frame_qkv": frame_qkv, "frame_out": frame_out, "global_gain": global_gain, "global_qkv": global_qkv, "global_out": global_out, "head_gain": head_gain, "head_proj": head_proj, "head_bias": head_bias, "head_conv": head_conv}


norm_eps = 1e-06
head_eps = 1e-05

def layer_norm(values, gain, epsilon):
    centre = values - lax.optimization_barrier(jnp.mean(values, axis=-1, keepdims=True))
    spread = lax.optimization_barrier(jnp.mean(centre * centre, axis=-1, keepdims=True))
    return centre * lax.rsqrt(spread + epsilon) * gain

def attend_head(triple):
    queries, keys_all, values_all = triple
    scores = jnp.dot(queries, keys_all.T, preferred_element_type=jnp.float32) * HD ** (-0.5)
    probs = jnp.exp(scores - lax.optimization_barrier(jnp.max(scores, axis=-1, keepdims=True)))
    mixed = jnp.dot(probs.astype(jnp.bfloat16), values_all, preferred_element_type=jnp.float32)
    return mixed / lax.optimization_barrier(jnp.sum(probs, axis=-1, keepdims=True))

def by_heads(matrix):
    return matrix.reshape(matrix.shape[0], HEADS, HD).transpose(1, 0, 2)

def attention(queries, keys_all, values_all):
    mixed = lax.map(attend_head, (by_heads(queries), by_heads(keys_all), by_heads(values_all)))
    return mixed.transpose(1, 0, 2).reshape(queries.shape[0], D).astype(jnp.bfloat16)

def attention_block(inputs, gain, qkv_weight, out_weight, wide):
    frames_now, per_frame = (inputs.shape[0], inputs.shape[1])
    normed = layer_norm(inputs.astype(jnp.float32), gain, norm_eps).astype(jnp.bfloat16)
    flattened = normed.reshape(frames_now * per_frame, D)
    query_rows = jnp.dot(flattened, qkv_weight[0], preferred_element_type=jnp.float32).astype(jnp.bfloat16)
    key_rows = jnp.dot(flattened, qkv_weight[1], preferred_element_type=jnp.float32).astype(jnp.bfloat16)
    value_rows = jnp.dot(flattened, qkv_weight[2], preferred_element_type=jnp.float32).astype(jnp.bfloat16)
    query_frames = query_rows.reshape(frames_now, per_frame, D)
    if wide:

        def one_frame(frame_queries):
            return attention(frame_queries, key_rows, value_rows)
        mixed = lax.map(one_frame, query_frames)
    else:

        def own_frame(triple):
            return attention(triple[0], triple[1], triple[2])
        mixed = lax.map(own_frame, (query_frames, key_rows.reshape(frames_now, per_frame, D), value_rows.reshape(frames_now, per_frame, D)))
    branch = jnp.dot(mixed.reshape(-1, D), out_weight, preferred_element_type=jnp.float32)
    merged = inputs.astype(jnp.float32).reshape(-1, D) + branch
    return merged.astype(jnp.bfloat16).reshape(inputs.shape)

def reference(tokens, frame_gain, frame_qkv, frame_out, global_gain, global_qkv, global_out, head_gain, head_proj, head_bias, head_conv):
    inputs = tokens.reshape(FRAMES, PR * PC, D)
    first = attention_block(inputs, frame_gain, frame_qkv, frame_out, False)
    second = attention_block(first, global_gain, global_qkv, global_out, True)
    stacked = jnp.concatenate([first.astype(jnp.float32), second.astype(jnp.float32)], axis=-1)
    normed = layer_norm(stacked, head_gain, head_eps).astype(jnp.bfloat16)
    projected = jnp.dot(normed.reshape(-1, 2 * D), head_proj, preferred_element_type=jnp.float32) + head_bias
    projected = projected.astype(jnp.bfloat16).reshape(FRAMES, PR, PC, CH)
    padded = jnp.pad(projected, ((0, 0), (1, 1), (1, 1), (0, 0)))
    totals = jnp.zeros((FRAMES, PR, PC, CH), jnp.float32)
    for offset_row in range(3):
        for offset_col in range(3):
            window = padded[:, offset_row:offset_row + PR, offset_col:offset_col + PC].astype(jnp.float32)
            totals = totals + jnp.einsum('frcx,xy->frcy', window, head_conv[offset_row, offset_col].astype(jnp.float32))
    return (second.reshape(FRAMES, PR, PC, D), totals.astype(jnp.bfloat16))
```

```python
import functools

import jax
import jax.numpy as jnp
from jax import lax
from jax.experimental import pallas as pl
from jax.experimental.pallas import tpu as pltpu
from jax.sharding import PartitionSpec as P

HD = 64


norm_eps = 1e-06
head_eps = 1e-05


def padded_2(block, sides, width):
    for axis, dim in sides:
        count = lax.axis_size(axis)
        forward = [(i, i + 1) for i in range(count - 1)]
        backward = [(target, source) for source, target in forward]
        low = lax.ppermute(
            lax.slice_in_dim(block, block.shape[dim] - width, None, axis=dim), axis, forward
        )
        high = lax.ppermute(lax.slice_in_dim(block, 0, width, axis=dim), axis, backward)
        block = jnp.concatenate([low, block, high], axis=dim)
    return block


def layer_norm(values, gain, epsilon):
    centre = values - jnp.mean(values, axis=-1, keepdims=True)
    spread = jnp.mean(centre * centre, axis=-1, keepdims=True)
    return centre * lax.rsqrt(spread + epsilon) * gain


def by_heads(matrix):
    return matrix.reshape(matrix.shape[0], matrix.shape[1] // HD, HD)


def attend_local(queries, keys_all, values_all):
    scores = jnp.einsum(
        "qhd,khd->qhk", by_heads(queries), by_heads(keys_all), preferred_element_type=jnp.float32
    ) * HD ** (-0.5)
    probs = jnp.exp(scores - jnp.max(scores, axis=-1, keepdims=True))
    mixed = jnp.einsum(
        "qhk,khd->qhd",
        probs.astype(jnp.bfloat16),
        by_heads(values_all),
        preferred_element_type=jnp.float32,
    )
    mixed = mixed / jnp.sum(probs, axis=-1)[..., None]
    return mixed.reshape(queries.shape).astype(jnp.bfloat16)


def key_step(local_rows, portion_rows):
    amount = portion_rows // local_rows
    best = 1
    for factor in range(1, amount + 1):
        if amount % factor == 0 and local_rows * factor <= max(local_rows, 1024):
            best = factor
    return local_rows * best


def fresh_carry(queries):
    heads_q = by_heads(queries)
    return (
        jnp.full(heads_q.shape[:2], -jnp.inf, jnp.float32),
        jnp.zeros(heads_q.shape[:2], jnp.float32),
        jnp.zeros(heads_q.shape, jnp.float32),
    )


def finish(carry, queries):
    return (carry[2] / carry[1][..., None]).reshape(queries.shape).astype(jnp.bfloat16)


def fold_keys(queries, carry, portions, local_rows):
    keys_in, values_in = portions
    step_rows = key_step(local_rows, keys_in.shape[0])
    heads_q = by_heads(queries)
    key_blocks = keys_in.reshape(-1, step_rows, keys_in.shape[1])
    value_blocks = values_in.reshape(-1, step_rows, values_in.shape[1])

    def absorb(states, blocks_pair):
        running_max, running_sum, weighted = states
        scores = jnp.einsum(
            "qhd,khd->qhk", heads_q, by_heads(blocks_pair[0]), preferred_element_type=jnp.float32
        ) * HD ** (-0.5)
        new_max = jnp.maximum(running_max, jnp.max(scores, axis=-1))
        decay = jnp.exp(running_max - new_max)
        probs = jnp.exp(scores - new_max[..., None])
        running_sum = running_sum * decay + jnp.sum(probs, axis=-1)
        weighted = weighted * decay[..., None] + jnp.einsum(
            "qhk,khd->qhd",
            probs.astype(jnp.bfloat16),
            by_heads(blocks_pair[1]),
            preferred_element_type=jnp.float32,
        )
        return ((new_max, running_sum, weighted), None)

    carry, ignored = lax.scan(absorb, carry, (key_blocks, value_blocks))
    return carry


def attention_block(inputs, gain, qkv_weight, out_weight, wide):
    normed = layer_norm(inputs.astype(jnp.float32), gain, norm_eps).astype(jnp.bfloat16)
    gathered = lax.all_gather(normed, "head", axis=1, tiled=True)
    flattened = gathered.reshape(-1, gathered.shape[-1])
    query_rows = jnp.dot(flattened, qkv_weight[0], preferred_element_type=jnp.float32).astype(
        jnp.bfloat16
    )
    key_rows = jnp.dot(flattened, qkv_weight[1], preferred_element_type=jnp.float32).astype(
        jnp.bfloat16
    )
    value_rows = jnp.dot(flattened, qkv_weight[2], preferred_element_type=jnp.float32).astype(
        jnp.bfloat16
    )
    if wide:
        carry = fold_keys(
            query_rows,
            fresh_carry(query_rows),
            (
                lax.all_gather(key_rows, ("seq", "band"), axis=0, tiled=True),
                lax.all_gather(value_rows, ("seq", "band"), axis=0, tiled=True),
            ),
            key_rows.shape[0],
        )
        attended = finish(carry, query_rows)
    else:
        keys_all, values_all = (
            lax.all_gather(key_rows, "band", axis=0, tiled=True),
            lax.all_gather(value_rows, "band", axis=0, tiled=True),
        )
        attended = attend_local(query_rows, keys_all, values_all)
    band_rows = inputs.shape[1] * inputs.shape[2]
    own_rows = lax.all_to_all(attended, "head", split_axis=0, concat_axis=1, tiled=True)
    branch = jnp.dot(
        own_rows,
        lax.all_gather(out_weight, "head", axis=0, tiled=True),
        preferred_element_type=jnp.float32,
    )
    merged = inputs.astype(jnp.float32).reshape(band_rows, -1) + branch
    return merged.astype(jnp.bfloat16).reshape(inputs.shape)


def on_device(
    tokens,
    frame_gain,
    frame_qkv,
    frame_out,
    global_gain,
    global_qkv,
    global_out,
    head_gain,
    head_proj,
    head_bias,
    head_conv,
):
    first = attention_block(tokens, frame_gain, frame_qkv, frame_out, False)
    second = attention_block(first, global_gain, global_qkv, global_out, True)
    band_height = tokens.shape[1]
    grid_width = tokens.shape[2]
    stacked = jnp.concatenate([first.astype(jnp.float32), second.astype(jnp.float32)], axis=-1)
    normed = layer_norm(stacked, head_gain, head_eps).astype(jnp.bfloat16)
    projected = (
        jnp.dot(
            normed.reshape(-1, stacked.shape[-1]), head_proj, preferred_element_type=jnp.float32
        )
        + head_bias
    )
    projected = projected.astype(jnp.bfloat16).reshape(
        tokens.shape[0], band_height, grid_width, head_proj.shape[1]
    )
    padded = padded_2(projected, ((("head", "band"), 1),), 1)
    padded = jnp.pad(padded, ((0, 0), (0, 0), (1, 1), (0, 0)))
    totals = jnp.zeros(projected.shape, jnp.float32)
    for offset_row in range(3):
        for offset_col in range(3):
            window = padded[
                :, offset_row : offset_row + band_height, offset_col : offset_col + grid_width
            ]
            totals = totals + jnp.einsum(
                "frcx,xy->frcy",
                window,
                head_conv[offset_row, offset_col],
                preferred_element_type=jnp.float32,
            )
    return (second, totals.astype(jnp.bfloat16))


BF = jnp.bfloat16
F32 = jnp.float32
TILE = 16


def up(count):
    return -(-count // TILE) * TILE


def mm(a, b):
    return jnp.dot(a, b, preferred_element_type=F32)


def swap(values):
    return pltpu.roll(values, HD, axis=1)


def scene_kernel(
    seq,
    real,
    width,
    tok,
    f_gain,
    f_qkv,
    f_out,
    g_gain,
    g_qkv,
    g_out,
    h_gain,
    h_proj,
    h_bias,
    h_conv,
    blocks_ref,
    feat_ref,
    toks,
    wf,
    wg,
    fo,
    go,
    wp,
    wc,
    q1,
    k1,
    v1,
    att,
    acc,
    normed,
    sqk,
    sv,
    rqk,
    rv,
    kk,
    vx,
    so,
    ro,
    a2,
    r2,
    pj,
    halo,
    xbuf,
    send,
    recv,
    local,
):
    s, z = lax.axis_index("scene"), lax.axis_index("seq")
    x, c = lax.axis_index("head"), lax.axis_index("band")
    rows, dim = tok.shape
    cols = wf.shape[2]
    pairs = cols // (2 * HD)
    frame = 4 * rows
    half = frame // 2
    peers = [None, (s, z, x, 1 - c), (s, z, 1 - x, c), (s, z, 1 - x, 1 - c)]

    def z_peer(offset):
        return (s, lax.rem(z + offset, seq), x, c)

    started = []

    def put(index, source, target, device):
        copy = pltpu.make_async_remote_copy(
            src_ref=source,
            dst_ref=target,
            send_sem=send.at[index],
            recv_sem=recv.at[index],
            device_id=device,
            device_id_type=pl.DeviceIdType.MESH,
        )
        copy.start()
        started.append(copy)
        return copy

    own_cols = pl.ds(pl.multiple_of(c * cols, cols), cols)
    other_cols = pl.ds(pl.multiple_of((1 - c) * cols, cols), cols)
    loads = [
        pltpu.make_async_copy(f_qkv.at[:, :, own_cols], wf, local.at[0]),
        pltpu.make_async_copy(f_out.at[own_cols], fo.at[0], local.at[1]),
        pltpu.make_async_copy(f_out.at[other_cols], fo.at[1], local.at[2]),
        pltpu.make_async_copy(g_qkv.at[:, :, own_cols], wg, local.at[3]),
        pltpu.make_async_copy(g_out.at[own_cols], go.at[0], local.at[4]),
        pltpu.make_async_copy(g_out.at[other_cols], go.at[1], local.at[5]),
        pltpu.make_async_copy(h_proj, wp, local.at[6]),
        pltpu.make_async_copy(h_conv, wc, local.at[7]),
    ]
    for load in loads:
        load.start()

    barrier = pltpu.get_barrier_semaphore()
    everyone = peers[1:] + [z_peer(d) for d in range(1, seq)]
    for device in everyone:
        pl.semaphore_signal(
            barrier, inc=1, device_id=device, device_id_type=pl.DeviceIdType.MESH
        )
    pl.semaphore_wait(barrier, len(everyone))

    T_CORE, T_X, T_FWD, F_X, F_FWD, G_X, G_FWD = range(7)
    A_CORE, A_X, A_FWD = 7, 7 + pairs, 7 + 2 * pairs
    ZQ = 7 + 3 * pairs
    ZV, ZO = ZQ + seq, ZQ + 2 * seq
    B2 = ZQ + 3 * seq
    HALO = B2 + 4

    tok_x = put(T_X, tok, toks.at[2], peers[2])
    tok_core = put(T_CORE, tok, toks.at[1], peers[1])
    fo_x = put(F_X, f_out.at[own_cols], fo.at[2], peers[2])

    block_row = lax.broadcasted_iota(jnp.int32, (rows, 1), 0)
    block_valid = block_row < real
    valid = jnp.concatenate([block_valid] * 4, axis=0)
    low = lax.broadcasted_iota(jnp.int32, (1, 2 * HD), 1) < HD

    def qkv1(slot, source):
        n = layer_norm(source[...].astype(F32), f_gain[...], norm_eps).astype(BF)
        at = pl.ds(slot * rows, rows)
        q1[at, :] = (mm(n, wf[0]).astype(BF) * HD ** (-0.5)).astype(BF)
        k1[at, :] = mm(n, wf[1]).astype(BF)
        v1[at, :] = jnp.where(block_valid, mm(n, wf[2]), 0.0).astype(BF)

    loads[0].wait()
    qkv1(0, tok)
    tok_core.wait_recv()
    qkv1(1, toks.at[1])
    tok_x.wait_recv()
    tok_fwd = put(T_FWD, toks.at[2], toks.at[3], peers[1])
    qkv1(2, toks.at[2])
    tok_fwd.wait_recv()
    qkv1(3, toks.at[3])

    att_core, att_x = [], []
    ones = jnp.where(valid, 1.0, 0.0).astype(BF)
    for p in range(pairs):
        at = pl.ds(p * 2 * HD, 2 * HD)
        qp, kp, vp = q1[:, at], k1[:, at], v1[:, at]
        outs = []
        for keep in (low, jnp.logical_not(low)):
            scores = lax.dot_general(
                jnp.where(keep, qp, jnp.zeros_like(qp)),
                kp,
                (((1,), (1,)), ((), ())),
                preferred_element_type=F32,
            )
            probs = jnp.exp(scores - jnp.max(scores, axis=-1, keepdims=True))
            outs.append(mm(probs.astype(BF), jnp.where(keep, vp, ones)))
        top = jnp.where(low, outs[0], outs[1])
        bottom = swap(jnp.where(low, outs[1], outs[0]))
        att[0, p] = (top / bottom).astype(BF)
        att_x.append(put(A_X + p, att.at[0, p], att.at[2, p], peers[2]))
        att_core.append(put(A_CORE + p, att.at[0, p], att.at[1, p], peers[1]))
    go_x = put(G_X, g_out.at[own_cols], go.at[2], peers[2])

    def gathered(group):
        parts = []
        for r in group:
            for p in range(pairs):
                parts.append(
                    jnp.concatenate(
                        [att[r, p, pl.ds((r ^ t) * rows, rows), :] for t in range(4)], axis=0
                    )
                )
        return jnp.concatenate(parts, axis=1)

    steps = dim // 256

    def column(i):
        return pl.ds(pl.multiple_of(i * 256, 256), 256)

    for load in loads[1:3]:
        load.wait()
    for copy in att_core:
        copy.wait_recv()
    lhs_near = gathered((0, 1))

    @pl.loop(0, steps)
    def _(i):
        at = column(i)
        weight = jnp.concatenate([fo[0, :, at], fo[1, :, at]], axis=0)
        base = jnp.concatenate(
            [tok[:, at]] + [toks[r, :, at] for r in (1, 2, 3)], axis=0
        ).astype(F32)
        acc[:, at] = base + mm(lhs_near, weight)

    fo_x.wait_recv()
    fo_fwd = put(F_FWD, fo.at[2], fo.at[3], peers[1])
    att_fwd = []
    for p in range(pairs):
        att_x[p].wait_recv()
        att_fwd.append(put(A_FWD + p, att.at[2, p], att.at[3, p], peers[1]))
    fo_fwd.wait_recv()
    for copy in att_fwd:
        copy.wait_recv()
    lhs_far = gathered((2, 3))

    @pl.loop(0, steps)
    def _(i):
        at = column(i)
        weight = jnp.concatenate([fo[2, :, at], fo[3, :, at]], axis=0)
        acc[:, at] += mm(lhs_far, weight)

    for t in range(4):
        at = pl.ds(t * rows, rows)
        first = acc[at, :].astype(BF).astype(F32)
        normed[at, :] = layer_norm(first, g_gain[...], norm_eps).astype(BF)
    loads[3].wait()
    n2 = normed[...]
    for p in range(pairs):
        at = pl.ds(p * 2 * HD, 2 * HD)
        qp = (mm(n2, wg[0, :, at]).astype(BF) * HD ** (-0.5)).astype(F32)
        kp = mm(n2, wg[1, :, at])
        vp = jnp.where(valid, mm(n2, wg[2, :, at]), 0.0)
        sqk[2 * p] = jnp.where(low, qp, swap(kp)).astype(BF)
        sqk[2 * p + 1] = jnp.where(low, swap(qp), kp).astype(BF)
        upper, under = vp[:half], vp[half:]
        sv[2 * p] = jnp.where(low, upper, swap(under)).astype(BF)
        sv[2 * p + 1] = jnp.where(low, swap(upper), under).astype(BF)

    z_copies = []
    for d in range(1, seq):
        to = lax.rem(z + d, seq)
        z_copies.append(put(ZQ + d, sqk.at[to], rqk.at[d], z_peer(d)))
        z_copies.append(put(ZV + d, sv.at[to], rv.at[d], z_peer(d)))
    rqk[0] = sqk[z]
    rv[0] = sv[z]

    go_x.wait_recv()
    go_fwd = put(G_FWD, go.at[2], go.at[3], peers[1])

    def arrange(d):
        at = pl.ds(d * frame, frame)
        kk[at, :] = swap(rqk[d].astype(F32)).astype(BF)
        packed = rv[d].astype(F32)
        spread = jnp.concatenate([packed, swap(packed)], axis=0)
        vx[at, :] = jnp.where(low, spread, jnp.where(valid, 1.0, 0.0)).astype(BF)

    arrange(0)
    for d in range(1, seq):
        z_copies[2 * d - 2].wait_recv()
        z_copies[2 * d - 1].wait_recv()
        arrange(d)

    def back(d):
        return pltpu.make_async_remote_copy(
            src_ref=so.at[d],
            dst_ref=ro.at[z],
            send_sem=send.at[ZO + d],
            recv_sem=recv.at[ZO + d],
            device_id=z_peer(seq - d),
            device_id_type=pl.DeviceIdType.MESH,
        )

    @pl.loop(1, seq + 1)
    def _(i):
        d = lax.rem(i, seq)
        keys, values = kk[...], vx[...]
        outs = []
        for part in range(2):
            qp = rqk[d, pl.ds(part * half, half), :]
            scores = lax.dot_general(
                jnp.where(low, qp, jnp.zeros_like(qp)),
                keys,
                (((1,), (1,)), ((), ())),
                preferred_element_type=F32,
            )
            probs = jnp.exp(scores - jnp.max(scores, axis=-1, keepdims=True))
            mixed = mm(probs.astype(BF), values)
            outs.append(mixed / jnp.where(low, swap(mixed), 1.0))
        so[d] = jnp.where(low, outs[0], swap(outs[1])).astype(BF)

        @pl.when(d > 0)
        def _():
            back(d).start()

    ro[z] = so[0]
    for d in range(1, seq):
        back(d).wait_recv()

    for p in range(pairs):
        at = pl.ds(p * 2 * HD, 2 * HD)
        even, odd = ro[2 * p].astype(F32), ro[2 * p + 1].astype(F32)
        a2[pl.ds(0, half), at] = jnp.where(low, even, swap(odd)).astype(BF)
        a2[pl.ds(half, half), at] = jnp.where(low, swap(even), odd).astype(BF)
    a2_copies = [
        put(B2 + r, a2.at[pl.ds(r * rows, rows)], r2.at[r], peers[r]) for r in (2, 3, 1)
    ]
    own = pl.ds(0, rows)
    first = acc[own, :].astype(BF).astype(F32)
    for load in loads[4:]:
        load.wait()
    go_fwd.wait_recv()
    branch = mm(a2[own, :], go[0])
    for copy in a2_copies:
        copy.wait_recv()
    for r in range(1, 4):
        branch = branch + mm(r2[r], go[r])
    second = (first + branch).astype(BF)
    blocks_ref[...] = second
    stacked = jnp.concatenate([first, second.astype(F32)], axis=-1)
    n3 = layer_norm(stacked, h_gain[...], head_eps).astype(BF)
    pj[...] = (mm(n3, wp[...]) + h_bias[...]).astype(BF)

    place = 2 * x + c
    after = lax.rem(place + 1, 4)
    before = lax.rem(place + 3, 4)

    def frame_peer(index):
        return (s, z, index // 2, lax.rem(index, 2))

    start = (real - width) // TILE * TILE
    slab = halo.shape[1]
    down = put(HALO, pj.at[pl.ds(start, rows - start)], halo.at[0, pl.ds(0, rows - start)], frame_peer(after))
    upward = put(HALO + 1, pj.at[pl.ds(0, slab)], halo.at[1], frame_peer(before))
    base = 8
    xbuf[...] = jnp.zeros_like(xbuf)
    xbuf[base + width : base + width + real, :] = pj[...].astype(F32)[:real]
    down.wait_recv()
    upward.wait_recv()
    skip = real - width - start
    lower = jnp.where(place > 0, halo[0].astype(F32), 0.0)
    upper = jnp.where(place < 3, halo[1].astype(F32), 0.0)
    xbuf[base : base + width, :] = lower[skip : skip + width]
    xbuf[base + width + real : base + 2 * width + real, :] = upper[:width]
    col = lax.rem(block_row, width)
    total = jnp.zeros(feat_ref.shape, F32)
    for i in range(3):
        for j in range(3):
            first_row = base + width * i + j - 1
            window = xbuf[first_row : first_row + rows, :]
            if j == 0:
                window = jnp.where(col > 0, window, 0.0)
            if j == 2:
                window = jnp.where(col < width - 1, window, 0.0)
            total = total + mm(window.astype(BF), wc[3 * i + j])
    feat_ref[...] = total.astype(BF)

    for copy in started:
        copy.wait_send()
    for d in range(1, seq):
        back(d).wait_send()


def scene_program(seq, *arrays):
    (tokens, f_gain, f_qkv, f_out, g_gain, g_qkv, g_out, h_gain, h_proj, h_bias, h_conv) = arrays
    height, width, dim = tokens.shape[1:]
    real = height * width
    rows = up(real)
    cols = f_qkv.shape[2] // 2
    pairs = cols // (2 * HD)
    channels = h_proj.shape[1]
    frame = 4 * rows
    half = frame // 2
    flat = tokens.reshape(real, dim)
    flat = jnp.concatenate([flat] + [flat[-1:]] * (rows - real), axis=0)
    vmem = pl.BlockSpec(memory_space=pltpu.VMEM)
    hbm = pl.BlockSpec(memory_space=pl.ANY)
    start = (real - width) // TILE * TILE
    slab = max(up(width), rows - start)
    copies = 7 + 3 * pairs + 3 * seq + 4 + 2
    blocks, features = pl.pallas_call(
        functools.partial(scene_kernel, seq, real, width),
        out_shape=(
            jax.ShapeDtypeStruct((rows, dim), BF),
            jax.ShapeDtypeStruct((rows, channels), BF),
        ),
        in_specs=[vmem, vmem, hbm, hbm, vmem, hbm, hbm, vmem, hbm, vmem, hbm],
        out_specs=(vmem, vmem),
        scratch_shapes=[
            pltpu.VMEM((4, rows, dim), BF),
            pltpu.VMEM((3, dim, cols), BF),
            pltpu.VMEM((3, dim, cols), BF),
            pltpu.VMEM((4, cols, dim), BF),
            pltpu.VMEM((4, cols, dim), BF),
            pltpu.VMEM(h_proj.shape, BF),
            pltpu.VMEM((9, channels, channels), BF),
            pltpu.VMEM((frame, cols), BF),
            pltpu.VMEM((frame, cols), BF),
            pltpu.VMEM((frame, cols), BF),
            pltpu.VMEM((4, pairs, frame, 2 * HD), BF),
            pltpu.VMEM((frame, dim), F32),
            pltpu.VMEM((frame, dim), BF),
            pltpu.VMEM((seq, frame, 2 * HD), BF),
            pltpu.VMEM((seq, half, 2 * HD), BF),
            pltpu.VMEM((seq, frame, 2 * HD), BF),
            pltpu.VMEM((seq, half, 2 * HD), BF),
            pltpu.VMEM((seq * frame, 2 * HD), BF),
            pltpu.VMEM((seq * frame, 2 * HD), BF),
            pltpu.VMEM((seq, half, 2 * HD), BF),
            pltpu.VMEM((seq, half, 2 * HD), BF),
            pltpu.VMEM((frame, cols), BF),
            pltpu.VMEM((4, rows, cols), BF),
            pltpu.VMEM((rows, channels), BF),
            pltpu.VMEM((2, slab, channels), BF),
            pltpu.VMEM((up(rows + 2 * width + 2 * TILE), channels), F32),
            pltpu.SemaphoreType.DMA((copies,)),
            pltpu.SemaphoreType.DMA((copies,)),
            pltpu.SemaphoreType.DMA((8,)),
        ],
        compiler_params=pltpu.CompilerParams(
            collective_id=0, has_side_effects=True, vmem_limit_bytes=48 * 2**20
        ),
    )(
        flat,
        f_gain.reshape(1, -1),
        f_qkv,
        f_out,
        g_gain.reshape(1, -1),
        g_qkv,
        g_out,
        h_gain.reshape(1, -1),
        h_proj,
        h_bias.reshape(1, -1),
        h_conv.reshape(9, channels, channels),
    )
    return (
        blocks[:real].reshape(tokens.shape),
        features[:real].reshape(1, height, width, channels),
    )


def routed(mesh, *arrays):
    sizes = mesh.shape
    frames, height, width = arrays[0].shape[:3]
    heads = arrays[2].shape[2] // HD
    fits = (
        sizes["head"] == 2
        and sizes["band"] == 2
        and frames == 1
        and heads == 2 * sizes["seq"]
        and sizes["seq"] % 2 == 0
        and height * width >= up(width)
    )
    if fits:
        return scene_program(sizes["seq"], *arrays)
    return on_device(*arrays)


def solution(mesh):
    return jax.shard_map(
        functools.partial(routed, mesh),
        mesh=mesh,
        in_specs=(
            P(("scene", "seq"), ("head", "band"), None, None),
            P(),
            P(None, None, "head"),
            P("head", None),
            P(),
            P(None, None, "head"),
            P("head", None),
            P(),
            P(),
            P(),
            P(),
        ),
        out_specs=(
            P(("scene", "seq"), ("head", "band"), None, None),
            P(("scene", "seq"), ("head", "band"), None, None),
        ),
        check_vma=False,
    )
```

```python
import functools

import jax
import jax.numpy as jnp
from jax import lax
from jax.experimental import pallas as pl
from jax.experimental.pallas import tpu as pltpu
from jax.sharding import PartitionSpec as P

HD = 64


norm_eps = 1e-06
head_eps = 1e-05


def padded_2(block, sides, width):
    for axis, dim in sides:
        count = lax.axis_size(axis)
        forward = [(i, i + 1) for i in range(count - 1)]
        backward = [(target, source) for source, target in forward]
        low = lax.ppermute(
            lax.slice_in_dim(block, block.shape[dim] - width, None, axis=dim), axis, forward
        )
        high = lax.ppermute(lax.slice_in_dim(block, 0, width, axis=dim), axis, backward)
        block = jnp.concatenate([low, block, high], axis=dim)
    return block


def layer_norm(values, gain, epsilon):
    centre = values - jnp.mean(values, axis=-1, keepdims=True)
    spread = jnp.mean(centre * centre, axis=-1, keepdims=True)
    return centre * lax.rsqrt(spread + epsilon) * gain


def by_heads(matrix):
    return matrix.reshape(matrix.shape[0], matrix.shape[1] // HD, HD)


def attend_local(queries, keys_all, values_all):
    scores = jnp.einsum(
        "qhd,khd->qhk", by_heads(queries), by_heads(keys_all), preferred_element_type=jnp.float32
    ) * HD ** (-0.5)
    probs = jnp.exp(scores - jnp.max(scores, axis=-1, keepdims=True))
    mixed = jnp.einsum(
        "qhk,khd->qhd",
        probs.astype(jnp.bfloat16),
        by_heads(values_all),
        preferred_element_type=jnp.float32,
    )
    mixed = mixed / jnp.sum(probs, axis=-1)[..., None]
    return mixed.reshape(queries.shape).astype(jnp.bfloat16)


def key_step(local_rows, portion_rows):
    amount = portion_rows // local_rows
    best = 1
    for factor in range(1, amount + 1):
        if amount % factor == 0 and local_rows * factor <= max(local_rows, 1024):
            best = factor
    return local_rows * best


def fresh_carry(queries):
    heads_q = by_heads(queries)
    return (
        jnp.full(heads_q.shape[:2], -jnp.inf, jnp.float32),
        jnp.zeros(heads_q.shape[:2], jnp.float32),
        jnp.zeros(heads_q.shape, jnp.float32),
    )


def finish(carry, queries):
    return (carry[2] / carry[1][..., None]).reshape(queries.shape).astype(jnp.bfloat16)


def fold_keys(queries, carry, portions, local_rows):
    keys_in, values_in = portions
    step_rows = key_step(local_rows, keys_in.shape[0])
    heads_q = by_heads(queries)
    key_blocks = keys_in.reshape(-1, step_rows, keys_in.shape[1])
    value_blocks = values_in.reshape(-1, step_rows, values_in.shape[1])

    def absorb(states, blocks_pair):
        running_max, running_sum, weighted = states
        scores = jnp.einsum(
            "qhd,khd->qhk", heads_q, by_heads(blocks_pair[0]), preferred_element_type=jnp.float32
        ) * HD ** (-0.5)
        new_max = jnp.maximum(running_max, jnp.max(scores, axis=-1))
        decay = jnp.exp(running_max - new_max)
        probs = jnp.exp(scores - new_max[..., None])
        running_sum = running_sum * decay + jnp.sum(probs, axis=-1)
        weighted = weighted * decay[..., None] + jnp.einsum(
            "qhk,khd->qhd",
            probs.astype(jnp.bfloat16),
            by_heads(blocks_pair[1]),
            preferred_element_type=jnp.float32,
        )
        return ((new_max, running_sum, weighted), None)

    carry, ignored = lax.scan(absorb, carry, (key_blocks, value_blocks))
    return carry


def attention_block(inputs, gain, qkv_weight, out_weight, wide):
    normed = layer_norm(inputs.astype(jnp.float32), gain, norm_eps).astype(jnp.bfloat16)
    gathered = lax.all_gather(normed, "head", axis=1, tiled=True)
    flattened = gathered.reshape(-1, gathered.shape[-1])
    query_rows = jnp.dot(flattened, qkv_weight[0], preferred_element_type=jnp.float32).astype(
        jnp.bfloat16
    )
    key_rows = jnp.dot(flattened, qkv_weight[1], preferred_element_type=jnp.float32).astype(
        jnp.bfloat16
    )
    value_rows = jnp.dot(flattened, qkv_weight[2], preferred_element_type=jnp.float32).astype(
        jnp.bfloat16
    )
    if wide:
        carry = fold_keys(
            query_rows,
            fresh_carry(query_rows),
            (
                lax.all_gather(key_rows, ("seq", "band"), axis=0, tiled=True),
                lax.all_gather(value_rows, ("seq", "band"), axis=0, tiled=True),
            ),
            key_rows.shape[0],
        )
        attended = finish(carry, query_rows)
    else:
        keys_all, values_all = (
            lax.all_gather(key_rows, "band", axis=0, tiled=True),
            lax.all_gather(value_rows, "band", axis=0, tiled=True),
        )
        attended = attend_local(query_rows, keys_all, values_all)
    band_rows = inputs.shape[1] * inputs.shape[2]
    own_rows = lax.all_to_all(attended, "head", split_axis=0, concat_axis=1, tiled=True)
    branch = jnp.dot(
        own_rows,
        lax.all_gather(out_weight, "head", axis=0, tiled=True),
        preferred_element_type=jnp.float32,
    )
    merged = inputs.astype(jnp.float32).reshape(band_rows, -1) + branch
    return merged.astype(jnp.bfloat16).reshape(inputs.shape)


def on_device(
    tokens,
    frame_gain,
    frame_qkv,
    frame_out,
    global_gain,
    global_qkv,
    global_out,
    head_gain,
    head_proj,
    head_bias,
    head_conv,
):
    first = attention_block(tokens, frame_gain, frame_qkv, frame_out, False)
    second = attention_block(first, global_gain, global_qkv, global_out, True)
    band_height = tokens.shape[1]
    grid_width = tokens.shape[2]
    stacked = jnp.concatenate([first.astype(jnp.float32), second.astype(jnp.float32)], axis=-1)
    normed = layer_norm(stacked, head_gain, head_eps).astype(jnp.bfloat16)
    projected = (
        jnp.dot(
            normed.reshape(-1, stacked.shape[-1]), head_proj, preferred_element_type=jnp.float32
        )
        + head_bias
    )
    projected = projected.astype(jnp.bfloat16).reshape(
        tokens.shape[0], band_height, grid_width, head_proj.shape[1]
    )
    padded = padded_2(projected, ((("head", "band"), 1),), 1)
    padded = jnp.pad(padded, ((0, 0), (0, 0), (1, 1), (0, 0)))
    totals = jnp.zeros(projected.shape, jnp.float32)
    for offset_row in range(3):
        for offset_col in range(3):
            window = padded[
                :, offset_row : offset_row + band_height, offset_col : offset_col + grid_width
            ]
            totals = totals + jnp.einsum(
                "frcx,xy->frcy",
                window,
                head_conv[offset_row, offset_col],
                preferred_element_type=jnp.float32,
            )
    return (second, totals.astype(jnp.bfloat16))


BF = jnp.bfloat16
F32 = jnp.float32
TILE = 16


def up(count):
    return -(-count // TILE) * TILE


def mm(a, b):
    return jnp.dot(a, b, preferred_element_type=F32)


def swap(values):
    return pltpu.roll(values, HD, axis=1)


def scene_kernel(
    seq,
    real,
    width,
    tok,
    f_gain,
    f_qkv,
    f_out,
    g_gain,
    g_qkv,
    g_out,
    h_gain,
    h_proj,
    h_bias,
    h_conv,
    blocks_ref,
    feat_ref,
    toks,
    wf,
    wg,
    fo,
    go,
    wp,
    wc,
    q1,
    k1,
    v1,
    att,
    acc,
    normed,
    sqk,
    sv,
    rqk,
    rv,
    kk,
    vx,
    so,
    ro,
    a2,
    r2,
    pj,
    halo,
    xbuf,
    send,
    recv,
    local,
):
    s, z = lax.axis_index("scene"), lax.axis_index("seq")
    x, c = lax.axis_index("head"), lax.axis_index("band")
    rows, dim = tok.shape
    cols = wf.shape[2]
    pairs = cols // (2 * HD)
    frame = 4 * rows
    half = frame // 2
    peers = [None, (s, z, x, 1 - c), (s, z, 1 - x, c), (s, z, 1 - x, 1 - c)]

    def z_peer(offset):
        return (s, lax.rem(z + offset, seq), x, c)

    started = []

    def put(index, source, target, device):
        copy = pltpu.make_async_remote_copy(
            src_ref=source,
            dst_ref=target,
            send_sem=send.at[index],
            recv_sem=recv.at[index],
            device_id=device,
            device_id_type=pl.DeviceIdType.MESH,
        )
        copy.start()
        started.append(copy)
        return copy

    own_cols = pl.ds(pl.multiple_of(c * cols, cols), cols)
    other_cols = pl.ds(pl.multiple_of((1 - c) * cols, cols), cols)
    loads = [
        pltpu.make_async_copy(f_qkv.at[:, :, own_cols], wf, local.at[0]),
        pltpu.make_async_copy(f_out.at[own_cols], fo.at[0], local.at[1]),
        pltpu.make_async_copy(f_out.at[other_cols], fo.at[1], local.at[2]),
        pltpu.make_async_copy(g_qkv.at[:, :, own_cols], wg, local.at[3]),
        pltpu.make_async_copy(g_out.at[own_cols], go.at[0], local.at[4]),
        pltpu.make_async_copy(g_out.at[other_cols], go.at[1], local.at[5]),
        pltpu.make_async_copy(h_proj, wp, local.at[6]),
        pltpu.make_async_copy(h_conv, wc, local.at[7]),
    ]
    for load in loads:
        load.start()

    barrier = pltpu.get_barrier_semaphore()
    everyone = peers[1:] + [z_peer(d) for d in range(1, seq)]
    for device in everyone:
        pl.semaphore_signal(
            barrier, inc=1, device_id=device, device_id_type=pl.DeviceIdType.MESH
        )
    pl.semaphore_wait(barrier, len(everyone))

    T_CORE, T_X, T_FWD, F_X, F_Z, F_FWD, G_X, G_FWD = 0, 1, 2, 3, 5, 7, 9, 10
    A_CORE, A_X, A_FWD = 11, 11 + pairs, 11 + 2 * pairs
    ZQ = 11 + 3 * pairs
    ZV, ZO = ZQ + seq, ZQ + 2 * seq
    B2 = ZQ + 3 * seq
    HALO = B2 + 4

    tok_x = put(T_X, tok, toks.at[2], peers[2])
    tok_core = put(T_CORE, tok, toks.at[1], peers[1])
    mine = lax.rem(z, 2)
    part = cols // 2
    chunk = part // 2

    def piece(owner, k):
        return pl.ds(pl.multiple_of(owner * part + k * chunk, chunk), chunk)

    fo_x = []
    for k in range(2):
        source = f_out.at[pl.ds(pl.multiple_of(c * cols + mine * part + k * chunk, chunk), chunk)]
        fo_x.append(put(F_X + k, source, fo.at[2, piece(mine, k)], peers[2]))

    block_row = lax.broadcasted_iota(jnp.int32, (rows, 1), 0)
    block_valid = block_row < real
    valid = jnp.concatenate([block_valid] * 4, axis=0)
    low = lax.broadcasted_iota(jnp.int32, (1, 2 * HD), 1) < HD

    def qkv1(slot, source):
        n = layer_norm(source[...].astype(F32), f_gain[...], norm_eps).astype(BF)
        at = pl.ds(slot * rows, rows)
        q1[at, :] = (mm(n, wf[0]).astype(BF) * HD ** (-0.5)).astype(BF)
        k1[at, :] = mm(n, wf[1]).astype(BF)
        v1[at, :] = jnp.where(block_valid, mm(n, wf[2]), 0.0).astype(BF)

    loads[0].wait()
    qkv1(0, tok)
    tok_core.wait_recv()
    qkv1(1, toks.at[1])
    tok_x.wait_recv()
    tok_fwd = put(T_FWD, toks.at[2], toks.at[3], peers[1])
    qkv1(2, toks.at[2])
    tok_fwd.wait_recv()
    qkv1(3, toks.at[3])

    att_core, att_x = [], []
    ones = jnp.where(valid, 1.0, 0.0).astype(BF)
    for p in range(pairs):
        at = pl.ds(p * 2 * HD, 2 * HD)
        qp, kp, vp = q1[:, at], k1[:, at], v1[:, at]
        outs = []
        for keep in (low, jnp.logical_not(low)):
            scores = lax.dot_general(
                jnp.where(keep, qp, jnp.zeros_like(qp)),
                kp,
                (((1,), (1,)), ((), ())),
                preferred_element_type=F32,
            )
            probs = jnp.exp(scores - jnp.max(scores, axis=-1, keepdims=True))
            outs.append(mm(probs.astype(BF), jnp.where(keep, vp, ones)))
        top = jnp.where(low, outs[0], outs[1])
        bottom = swap(jnp.where(low, outs[1], outs[0]))
        att[0, p] = (top / bottom).astype(BF)
        att_x.append(put(A_X + p, att.at[0, p], att.at[2, p], peers[2]))
        att_core.append(put(A_CORE + p, att.at[0, p], att.at[1, p], peers[1]))
    pair_peer = (s, z + 1 - 2 * mine, x, c)
    mine_rows = pl.ds(pl.multiple_of(mine * part, part), part)
    pair_rows = pl.ds(pl.multiple_of((1 - mine) * part, part), part)
    fo_z = []
    for k in range(2):
        fo_x[k].wait_recv()
        at = piece(mine, k)
        fo_z.append(put(F_Z + k, fo.at[2, at], fo.at[2, at], pair_peer))
    fo_fwd = [put(F_FWD, fo.at[2, mine_rows], fo.at[3, mine_rows], peers[1])]
    go_x = put(G_X, g_out.at[own_cols], go.at[2], peers[2])

    def gathered(group):
        parts = []
        for r in group:
            for p in range(pairs):
                parts.append(
                    jnp.concatenate(
                        [att[r, p, pl.ds((r ^ t) * rows, rows), :] for t in range(4)], axis=0
                    )
                )
        return jnp.concatenate(parts, axis=1)

    steps = dim // 256

    def column(i):
        return pl.ds(pl.multiple_of(i * 256, 256), 256)

    for load in loads[1:3]:
        load.wait()
    for copy in att_core:
        copy.wait_recv()
    lhs_near = gathered((0, 1))

    @pl.loop(0, steps)
    def _(i):
        at = column(i)
        weight = jnp.concatenate([fo[0, :, at], fo[1, :, at]], axis=0)
        base = jnp.concatenate(
            [tok[:, at]] + [toks[r, :, at] for r in (1, 2, 3)], axis=0
        ).astype(F32)
        acc[:, at] = base + mm(lhs_near, weight)

    for copy in fo_z:
        copy.wait_recv()
    fo_fwd.append(put(F_FWD + 1, fo.at[2, pair_rows], fo.at[3, pair_rows], peers[1]))
    att_fwd = []
    for p in range(pairs):
        att_x[p].wait_recv()
        att_fwd.append(put(A_FWD + p, att.at[2, p], att.at[3, p], peers[1]))
    for copy in fo_fwd + att_fwd:
        copy.wait_recv()
    lhs_far = gathered((2, 3))

    @pl.loop(0, steps)
    def _(i):
        at = column(i)
        weight = jnp.concatenate([fo[2, :, at], fo[3, :, at]], axis=0)
        acc[:, at] += mm(lhs_far, weight)

    for t in range(4):
        at = pl.ds(t * rows, rows)
        first = acc[at, :].astype(BF).astype(F32)
        normed[at, :] = layer_norm(first, g_gain[...], norm_eps).astype(BF)
    loads[3].wait()
    n2 = normed[...]
    for p in range(pairs):
        at = pl.ds(p * 2 * HD, 2 * HD)
        qp = (mm(n2, wg[0, :, at]).astype(BF) * HD ** (-0.5)).astype(F32)
        kp = mm(n2, wg[1, :, at])
        vp = jnp.where(valid, mm(n2, wg[2, :, at]), 0.0)
        sqk[2 * p] = jnp.where(low, qp, swap(kp)).astype(BF)
        sqk[2 * p + 1] = jnp.where(low, swap(qp), kp).astype(BF)
        upper, under = vp[:half], vp[half:]
        sv[2 * p] = jnp.where(low, upper, swap(under)).astype(BF)
        sv[2 * p + 1] = jnp.where(low, swap(upper), under).astype(BF)

    z_copies = []
    for d in range(1, seq):
        to = lax.rem(z + d, seq)
        z_copies.append(put(ZQ + d, sqk.at[to], rqk.at[d], z_peer(d)))
        z_copies.append(put(ZV + d, sv.at[to], rv.at[d], z_peer(d)))
    rqk[0] = sqk[z]
    rv[0] = sv[z]

    go_x.wait_recv()
    go_fwd = put(G_FWD, go.at[2], go.at[3], peers[1])

    def arrange(d):
        at = pl.ds(d * frame, frame)
        kk[at, :] = swap(rqk[d].astype(F32)).astype(BF)
        packed = rv[d].astype(F32)
        spread = jnp.concatenate([packed, swap(packed)], axis=0)
        vx[at, :] = jnp.where(low, spread, jnp.where(valid, 1.0, 0.0)).astype(BF)

    arrange(0)
    for d in range(1, seq):
        z_copies[2 * d - 2].wait_recv()
        z_copies[2 * d - 1].wait_recv()
        arrange(d)

    def back(d):
        return pltpu.make_async_remote_copy(
            src_ref=so.at[d],
            dst_ref=ro.at[z],
            send_sem=send.at[ZO + d],
            recv_sem=recv.at[ZO + d],
            device_id=z_peer(seq - d),
            device_id_type=pl.DeviceIdType.MESH,
        )

    @pl.loop(1, seq + 1)
    def _(i):
        d = lax.rem(i, seq)
        keys, values = kk[...], vx[...]
        outs = []
        for part in range(2):
            qp = rqk[d, pl.ds(part * half, half), :]
            scores = lax.dot_general(
                jnp.where(low, qp, jnp.zeros_like(qp)),
                keys,
                (((1,), (1,)), ((), ())),
                preferred_element_type=F32,
            )
            probs = jnp.exp(scores - jnp.max(scores, axis=-1, keepdims=True))
            mixed = mm(probs.astype(BF), values)
            outs.append(mixed / jnp.where(low, swap(mixed), 1.0))
        so[d] = jnp.where(low, outs[0], swap(outs[1])).astype(BF)

        @pl.when(d > 0)
        def _():
            back(d).start()

    ro[z] = so[0]
    for d in range(1, seq):
        back(d).wait_recv()

    for p in range(pairs):
        at = pl.ds(p * 2 * HD, 2 * HD)
        even, odd = ro[2 * p].astype(F32), ro[2 * p + 1].astype(F32)
        a2[pl.ds(0, half), at] = jnp.where(low, even, swap(odd)).astype(BF)
        a2[pl.ds(half, half), at] = jnp.where(low, swap(even), odd).astype(BF)
    a2_copies = [
        put(B2 + r, a2.at[pl.ds(r * rows, rows)], r2.at[r], peers[r]) for r in (2, 3, 1)
    ]
    own = pl.ds(0, rows)
    first = acc[own, :].astype(BF).astype(F32)
    for load in loads[4:]:
        load.wait()
    go_fwd.wait_recv()
    branch = mm(a2[own, :], go[0])
    for copy in a2_copies:
        copy.wait_recv()
    for r in range(1, 4):
        branch = branch + mm(r2[r], go[r])
    second = (first + branch).astype(BF)
    blocks_ref[...] = second
    stacked = jnp.concatenate([first, second.astype(F32)], axis=-1)
    n3 = layer_norm(stacked, h_gain[...], head_eps).astype(BF)
    pj[...] = (mm(n3, wp[...]) + h_bias[...]).astype(BF)

    place = 2 * x + c
    after = lax.rem(place + 1, 4)
    before = lax.rem(place + 3, 4)

    def frame_peer(index):
        return (s, z, index // 2, lax.rem(index, 2))

    start = (real - width) // TILE * TILE
    slab = halo.shape[1]
    down = put(HALO, pj.at[pl.ds(start, rows - start)], halo.at[0, pl.ds(0, rows - start)], frame_peer(after))
    upward = put(HALO + 1, pj.at[pl.ds(0, slab)], halo.at[1], frame_peer(before))
    base = 8
    xbuf[...] = jnp.zeros_like(xbuf)
    xbuf[base + width : base + width + real, :] = pj[...].astype(F32)[:real]
    down.wait_recv()
    upward.wait_recv()
    skip = real - width - start
    lower = jnp.where(place > 0, halo[0].astype(F32), 0.0)
    upper = jnp.where(place < 3, halo[1].astype(F32), 0.0)
    xbuf[base : base + width, :] = lower[skip : skip + width]
    xbuf[base + width + real : base + 2 * width + real, :] = upper[:width]
    col = lax.rem(block_row, width)
    total = jnp.zeros(feat_ref.shape, F32)
    for i in range(3):
        for j in range(3):
            first_row = base + width * i + j - 1
            window = xbuf[first_row : first_row + rows, :]
            if j == 0:
                window = jnp.where(col > 0, window, 0.0)
            if j == 2:
                window = jnp.where(col < width - 1, window, 0.0)
            total = total + mm(window.astype(BF), wc[3 * i + j])
    feat_ref[...] = total.astype(BF)

    for copy in started:
        copy.wait_send()
    for d in range(1, seq):
        back(d).wait_send()


def scene_program(seq, *arrays):
    (tokens, f_gain, f_qkv, f_out, g_gain, g_qkv, g_out, h_gain, h_proj, h_bias, h_conv) = arrays
    height, width, dim = tokens.shape[1:]
    real = height * width
    rows = up(real)
    cols = f_qkv.shape[2] // 2
    pairs = cols // (2 * HD)
    channels = h_proj.shape[1]
    frame = 4 * rows
    half = frame // 2
    flat = tokens.reshape(real, dim)
    flat = jnp.concatenate([flat] + [flat[-1:]] * (rows - real), axis=0)
    vmem = pl.BlockSpec(memory_space=pltpu.VMEM)
    hbm = pl.BlockSpec(memory_space=pl.ANY)
    start = (real - width) // TILE * TILE
    slab = max(up(width), rows - start)
    copies = 11 + 3 * pairs + 3 * seq + 4 + 2
    blocks, features = pl.pallas_call(
        functools.partial(scene_kernel, seq, real, width),
        out_shape=(
            jax.ShapeDtypeStruct((rows, dim), BF),
            jax.ShapeDtypeStruct((rows, channels), BF),
        ),
        in_specs=[vmem, vmem, hbm, hbm, vmem, hbm, hbm, vmem, hbm, vmem, hbm],
        out_specs=(vmem, vmem),
        scratch_shapes=[
            pltpu.VMEM((4, rows, dim), BF),
            pltpu.VMEM((3, dim, cols), BF),
            pltpu.VMEM((3, dim, cols), BF),
            pltpu.VMEM((4, cols, dim), BF),
            pltpu.VMEM((4, cols, dim), BF),
            pltpu.VMEM(h_proj.shape, BF),
            pltpu.VMEM((9, channels, channels), BF),
            pltpu.VMEM((frame, cols), BF),
            pltpu.VMEM((frame, cols), BF),
            pltpu.VMEM((frame, cols), BF),
            pltpu.VMEM((4, pairs, frame, 2 * HD), BF),
            pltpu.VMEM((frame, dim), F32),
            pltpu.VMEM((frame, dim), BF),
            pltpu.VMEM((seq, frame, 2 * HD), BF),
            pltpu.VMEM((seq, half, 2 * HD), BF),
            pltpu.VMEM((seq, frame, 2 * HD), BF),
            pltpu.VMEM((seq, half, 2 * HD), BF),
            pltpu.VMEM((seq * frame, 2 * HD), BF),
            pltpu.VMEM((seq * frame, 2 * HD), BF),
            pltpu.VMEM((seq, half, 2 * HD), BF),
            pltpu.VMEM((seq, half, 2 * HD), BF),
            pltpu.VMEM((frame, cols), BF),
            pltpu.VMEM((4, rows, cols), BF),
            pltpu.VMEM((rows, channels), BF),
            pltpu.VMEM((2, slab, channels), BF),
            pltpu.VMEM((up(rows + 2 * width + 2 * TILE), channels), F32),
            pltpu.SemaphoreType.DMA((copies,)),
            pltpu.SemaphoreType.DMA((copies,)),
            pltpu.SemaphoreType.DMA((8,)),
        ],
        compiler_params=pltpu.CompilerParams(
            collective_id=0, has_side_effects=True
        ),
    )(
        flat,
        f_gain.reshape(1, -1),
        f_qkv,
        f_out,
        g_gain.reshape(1, -1),
        g_qkv,
        g_out,
        h_gain.reshape(1, -1),
        h_proj,
        h_bias.reshape(1, -1),
        h_conv.reshape(9, channels, channels),
    )
    return (
        blocks[:real].reshape(tokens.shape),
        features[:real].reshape(1, height, width, channels),
    )


def routed(mesh, *arrays):
    sizes = mesh.shape
    frames, height, width = arrays[0].shape[:3]
    heads = arrays[2].shape[2] // HD
    fits = (
        sizes["head"] == 2
        and sizes["band"] == 2
        and frames == 1
        and heads == 2 * sizes["seq"]
        and sizes["seq"] % 2 == 0
        and arrays[2].shape[2] // 2 % (4 * TILE) == 0
        and height * width >= up(width)
    )
    if fits:
        return scene_program(sizes["seq"], *arrays)
    return on_device(*arrays)


def solution(mesh):
    return jax.shard_map(
        functools.partial(routed, mesh),
        mesh=mesh,
        in_specs=(
            P(("scene", "seq"), ("head", "band"), None, None),
            P(),
            P(None, None, "head"),
            P("head", None),
            P(),
            P(None, None, "head"),
            P("head", None),
            P(),
            P(),
            P(),
            P(),
        ),
        out_specs=(
            P(("scene", "seq"), ("head", "band"), None, None),
            P(("scene", "seq"), ("head", "band"), None, None),
        ),
        check_vma=False,
    )
```
